32 devices in a mesh: groups: 2 (over y), seq: 16 (over z, x, core).
Axes of the slice: x: 2, y: 2, z: 4, core: 2. Of those that a mesh axis runs over, the one named last changes fastest.
Arguments:
- residual: bfloat16 [8192, 1024], P(('groups', 'seq')), parts along dimension 0, may hold values from -6 to 6
- layer_queries: bfloat16 [8192, 512], P(('groups', 'seq')), parts along dimension 0, may hold values from -200 to 200
- layer_keyvals: bfloat16 [8192, 256], P(('groups', 'seq')), parts along dimension 0, may hold values from -8 to 8
- head_window_extent: int32 [8], replicated, may hold values from 32 to 256, as said below
- block_mask: int32 [16, 4], P('seq'), may hold values 0 or 1
- first_out: bfloat16 [512, 1024], replicated, may hold values from -1 to 1
- second_query: bfloat16 [1024, 512], replicated, may hold values from -12 to 12
- second_keyval: bfloat16 [1024, 256], replicated, may hold values from -1 to 1
- second_out: bfloat16 [512, 1024], replicated, may hold values from -1 to 1
Outputs:
- layer_output: bfloat16 [8192, 1024], P(('groups', 'seq')), parts along dimension 0
The draws below stay inside these ranges and needn't reach their ends.
There are 2 independent parts, one for each index of `groups`. The reference program is written for one: setup_inputs(seed, part) draws one part's arguments, and reference() takes and returns one part's arrays. A program takes and returns all parts, laid end to end along the dimension named above; an argument that names none is the same for every part. Nothing has to cross between parts.
Inputs may be any that keep to these rules, and one draw needn't show every extreme that they name: `head_window_extent`: per head; some head has exactly 256 and some exactly 32.
All inputs are finite; a program needn't handle non-finite values. No bound on the sum of `block_mask` on one device may be relied on, other than what follows from the above.
Results may differ from the reference program's by a relative error of at most 0.0065.
Values may be sent and summed in bfloat16 or wider, within the bound.
A program may use at most 64 MiB of HBM per device.

```python
import jax
import jax.numpy as jnp
from jax import lax

MODEL_WIDTH = 1024
QUERY_HEADS = 8
KEY_VALUE_HEADS = 2
HEAD_SIZE = 64
TOK_DEV = 256
WIN = 256
LEVELS = 4
NB = 16
SEQUENCE_TOKENS = 4096


def draw_pair(key):
    key_q, random_key_keys = jax.random.split(jax.random.fold_in(key, 11), 2)
    query_matrix = jnp.clip(jax.random.normal(key_q, (SEQUENCE_TOKENS, QUERY_HEADS * HEAD_SIZE), jnp.float32), -6.0, 6.0)
    key_value_pairs = jnp.clip(jax.random.normal(random_key_keys, (SEQUENCE_TOKENS, 2 * KEY_VALUE_HEADS * HEAD_SIZE), jnp.float32), -6.0, 6.0)
    return (query_matrix, key_value_pairs)


def draw_layer_queries(key, part):
    return draw_pair(key)[0].astype(jnp.bfloat16)


def draw_layer_keyvals(key, part):
    return draw_pair(key)[1].astype(jnp.bfloat16)


def draw_head_window_extent(key, part):
    key_p, key_r = jax.random.split(jax.random.fold_in(key, 31))
    order = jax.random.permutation(key_p, QUERY_HEADS)
    window_extent = jax.random.randint(key_r, (QUERY_HEADS,), WIN // 8, WIN + 1)
    window_extent = window_extent.at[order[0]].set(WIN).at[order[1]].set(WIN // 8)
    return window_extent.astype(jnp.int32)


def draw_projections(key):
    key_q, random_key_keys = jax.random.split(jax.random.fold_in(key, 23), 2)
    w_query = jnp.clip(jax.random.normal(key_q, (MODEL_WIDTH, QUERY_HEADS * HEAD_SIZE), jnp.float32), -6.0, 6.0) * MODEL_WIDTH ** (-0.5)
    key_value_weight = jnp.clip(jax.random.normal(random_key_keys, (MODEL_WIDTH, 2 * KEY_VALUE_HEADS * HEAD_SIZE), jnp.float32), -6.0, 6.0) * MODEL_WIDTH ** (-0.5)
    return (w_query, key_value_weight)


def draw_second_query(key, part):
    return draw_projections(key)[0].astype(jnp.bfloat16)


def draw_second_keyval(key, part):
    return draw_projections(key)[1].astype(jnp.bfloat16)


def set_ends(entries, stream_key, least, largest):
    longest = entries.shape.index(max(entries.shape))
    spots = []
    for shift in (0, 1):
        where = [jax.random.randint(jax.random.fold_in(stream_key, axis), (), 0, length) for axis, length in enumerate(entries.shape)]
        where[longest] = (where[longest] + shift) % entries.shape[longest]
        spots.append(tuple(where))
    return entries.at[spots[0]].set(least).at[spots[1]].set(largest)


def level_of(rng, extent, pieces, least, largest):
    def one(axis_at, parts):
        heights = jax.random.uniform(jax.random.fold_in(jax.random.fold_in(rng, 6), axis_at), (parts,), jnp.float32, least / len(pieces), largest / len(pieces))
        return jnp.repeat(jnp.exp(heights), extent[axis_at] // parts).reshape((-1,) + (1,) * (len(extent) - axis_at - 1))

    level = one(*pieces[0])
    for cut in pieces[1:]:
        level = level * one(*cut)
    return level


def centred(rng, dims, scale, most, cuts=(), kind=jnp.bfloat16):
    entries = scale * jax.random.normal(rng, dims, jnp.float32)
    if cuts:
        entries = entries * level_of(rng, dims, cuts, -0.22, 0.18)
    return jnp.clip(entries, -most, most).astype(kind)


def setup_inputs(seed: int = 0, part: int = 0) -> dict:
    keys = jax.random.split(jax.random.key(seed), 10)
    part_splits = jax.random.split(jax.random.fold_in(keys[9], part), 10)
    residual = centred(part_splits[0], (SEQUENCE_TOKENS, MODEL_WIDTH), 1.0, 6.0, ((0, 16),))
    layer_queries = draw_layer_queries(jax.random.fold_in(jax.random.fold_in(keys[9], part), 71), part)
    layer_keyvals = draw_layer_keyvals(jax.random.fold_in(jax.random.fold_in(keys[9], part), 71), part)
    head_window_extent = draw_head_window_extent(jax.random.fold_in(keys[9], 71), part)
    block_mask = set_ends((jax.random.randint(keys[4], (NB, LEVELS), 0, 4) < 3).astype(jnp.int32), jax.random.fold_in(keys[4], 1), 0, 1)
    first_out = centred(keys[5], (QUERY_HEADS * HEAD_SIZE, MODEL_WIDTH), (QUERY_HEADS * HEAD_SIZE // 16) ** -0.5, 1.0)
    second_query = draw_second_query(jax.random.fold_in(keys[9], 71), part)
    second_keyval = draw_second_keyval(jax.random.fold_in(keys[9], 71), part)
    second_out = centred(keys[8], (QUERY_HEADS * HEAD_SIZE, MODEL_WIDTH), (QUERY_HEADS * HEAD_SIZE // 16) ** -0.5, 1.0)
    return dict(residual=residual, layer_queries=layer_queries, layer_keyvals=layer_keyvals, head_window_extent=head_window_extent, block_mask=block_mask, first_out=first_out, second_query=second_query, second_keyval=second_keyval, second_out=second_out)


def norm_rows(hidden):
    values = hidden.astype(jnp.float32)
    scale = lax.rsqrt(lax.optimization_barrier(jnp.mean(values * values, axis=-1, keepdims=True)) + 1e-05)
    return (values * scale).astype(jnp.bfloat16)

def attend_rows(query_matrix, key_row_matrix, value_row_matrix, allowed):
    count_of_rows = query_matrix.shape[0]
    count_of_keys = key_row_matrix.shape[0]
    heads_per_group = QUERY_HEADS // KEY_VALUE_HEADS
    query_head_rows = query_matrix.reshape(count_of_rows, KEY_VALUE_HEADS, heads_per_group, HEAD_SIZE).astype(jnp.float32)
    key_head_rows = key_row_matrix.reshape(count_of_keys, KEY_VALUE_HEADS, HEAD_SIZE).astype(jnp.float32)
    value_head_rows = value_row_matrix.reshape(count_of_keys, KEY_VALUE_HEADS, HEAD_SIZE).astype(jnp.float32)
    scores = jnp.einsum('rkgd,jkd->kgrj', query_head_rows, key_head_rows) * HEAD_SIZE ** (-0.5)
    scores = jnp.where(allowed, scores, -1e+30)
    row_max = lax.optimization_barrier(jnp.max(scores, axis=-1, keepdims=True))
    weights = jnp.where(allowed, jnp.exp(scores - row_max), 0.0)
    shares = (weights / lax.optimization_barrier(jnp.sum(weights, axis=-1, keepdims=True))).astype(jnp.bfloat16)
    mixture = jnp.einsum('kgrj,jkd->rkgd', shares.astype(jnp.float32), value_head_rows)
    return mixture.reshape(count_of_rows, QUERY_HEADS * HEAD_SIZE).astype(jnp.bfloat16)

def reference(residual, layer_queries, layer_keyvals, head_window_extent, block_mask, first_out, second_query, second_keyval, second_out):
    key_value_width = KEY_VALUE_HEADS * HEAD_SIZE
    heads_per_group = QUERY_HEADS // KEY_VALUE_HEADS
    padded = jnp.pad(layer_keyvals, ((WIN, WIN), (0, 0)))
    window_extent = head_window_extent.reshape(KEY_VALUE_HEADS, heads_per_group, 1, 1)

    def window_block(block):
        first_row = block * TOK_DEV
        query_part = lax.dynamic_slice_in_dim(layer_queries, first_row, TOK_DEV, 0)
        key_portion = lax.dynamic_slice_in_dim(padded, first_row, TOK_DEV + 2 * WIN, 0)
        query_pos = first_row + jnp.arange(TOK_DEV, dtype=jnp.int32)
        key_pos = first_row - WIN + jnp.arange(TOK_DEV + 2 * WIN, dtype=jnp.int32)
        inside = (key_pos >= 0) & (key_pos < SEQUENCE_TOKENS)
        distance = jnp.abs(query_pos[:, None] - key_pos[None, :])
        allowed = (distance[None, None] <= window_extent) & inside[None, None, None, :]
        return attend_rows(query_part, key_portion[:, :key_value_width], key_portion[:, key_value_width:], allowed)
    attended = lax.map(window_block, jnp.arange(NB, dtype=jnp.int32)).reshape(SEQUENCE_TOKENS, QUERY_HEADS * HEAD_SIZE)
    hidden = (jnp.dot(attended, first_out, preferred_element_type=jnp.float32) + residual.astype(jnp.float32)).astype(jnp.bfloat16)
    normed = norm_rows(hidden)
    queries_two = jnp.dot(normed, second_query, preferred_element_type=jnp.float32).astype(jnp.bfloat16)
    keyvals_two = jnp.dot(normed, second_keyval, preferred_element_type=jnp.float32).astype(jnp.bfloat16)
    kv_blocks = keyvals_two.reshape(NB, TOK_DEV, 2 * key_value_width)
    level_bits = jnp.left_shift(jnp.ones((LEVELS,), jnp.int32), jnp.arange(LEVELS, dtype=jnp.int32))

    def butterfly_block(block):
        partners = jnp.bitwise_xor(block, level_bits)
        own_rows = kv_blocks[block]
        other_rows = kv_blocks[partners].reshape(LEVELS * TOK_DEV, 2 * key_value_width)
        key_portion = jnp.concatenate([own_rows, other_rows], axis=0)
        flags = jnp.concatenate([jnp.ones((1,), jnp.bool_), block_mask[block] == 1])
        allowed = jnp.repeat(flags, TOK_DEV)[None, None, None, :]
        query_part = lax.dynamic_slice_in_dim(queries_two, block * TOK_DEV, TOK_DEV, 0)
        return attend_rows(query_part, key_portion[:, :key_value_width], key_portion[:, key_value_width:], allowed)
    second = lax.map(butterfly_block, jnp.arange(NB, dtype=jnp.int32)).reshape(SEQUENCE_TOKENS, QUERY_HEADS * HEAD_SIZE)
    output = jnp.dot(second, second_out, preferred_element_type=jnp.float32) + hidden.astype(jnp.float32)
    return output.astype(jnp.bfloat16)
```

```python
import functools

import jax
import jax.numpy as jnp
from jax import lax
from jax.experimental import pallas as pl
from jax.experimental.pallas import tpu as pltpu
from jax.sharding import PartitionSpec as P

QUERY_HEADS = 8
HEAD_SIZE = 64
MESH = pl.DeviceIdType.MESH
HIDE = -1e30
NT = (((1,), (1,)), ((), ()))


def dot_nt(a, b):
    return lax.dot_general(a, b, NT, preferred_element_type=jnp.float32)


def dot(a, b):
    return jnp.dot(a, b, preferred_element_type=jnp.float32)


def low_half(shape):
    return lax.broadcasted_iota(jnp.int32, shape, 1) < HEAD_SIZE


def rolled(x):
    return jnp.concatenate([x[:, HEAD_SIZE:], x[:, :HEAD_SIZE]], axis=1)


def spread(keys, values, ones, kx, vx, slot):
    low = low_half(keys.shape)
    none = jnp.zeros_like(keys)
    keys = keys * jnp.bfloat16(HEAD_SIZE ** (-0.5))
    first, second = jnp.where(low, keys, none), jnp.where(low, none, keys)
    kx[slot, 0, 0] = first
    kx[slot, 0, 1] = rolled(first)
    kx[slot, 1, 0] = rolled(second)
    kx[slot, 1, 1] = second
    first, second = jnp.where(low, values, ones), jnp.where(low, ones, values)
    vx[slot, 0, 0] = first
    vx[slot, 0, 1] = rolled(first)
    vx[slot, 1, 0] = rolled(second)
    vx[slot, 1, 1] = second


def row_max(parts):
    top = jnp.max(parts[0], axis=1, keepdims=True)
    for part in parts[1:]:
        top = jnp.maximum(top, jnp.max(part, axis=1, keepdims=True))
    return top


def weight(scores, top):
    return jnp.exp((scores - top).astype(jnp.bfloat16))


def joined(even, odd):
    low = low_half(even.shape)
    return (jnp.where(low, even, odd) / rolled(jnp.where(low, odd, even))).astype(jnp.bfloat16)


def body(
    n,
    levels,
    q_hbm,
    kv_hbm,
    res_hbm,
    extent,
    mask,
    wo1_hbm,
    wq2_hbm,
    wkv2_hbm,
    wo2_hbm,
    out_hbm,
    q,
    kv,
    halo,
    res,
    wo1,
    wq2,
    wkv2,
    wo2,
    kv2,
    kv2_in,
    kx,
    vx,
    tops,
    accs,
    att,
    hid,
    out,
    local_sem,
    send_sem,
    recv_sem,
):
    rows = q.shape[0]
    half = rows // 2
    pairs = q.shape[1] // (2 * HEAD_SIZE)
    per_group = pairs // 2
    me = lax.axis_index("seq")
    loads = [
        pltpu.make_async_copy(src, dst, local_sem.at[i])
        for i, (src, dst) in enumerate(
            (
                (kv_hbm, kv),
                (q_hbm, q),
                (wo1_hbm, wo1),
                (res_hbm, res),
                (wkv2_hbm, wkv2),
                (wq2_hbm, wq2),
                (wo2_hbm, wo2),
            )
        )
    ]
    barrier = pltpu.get_barrier_semaphore()
    has_left, has_right = me > 0, me < n - 1

    @pl.when(has_left)
    def _():
        pl.semaphore_signal(barrier, inc=1, device_id={"seq": me - 1}, device_id_type=MESH)

    @pl.when(has_right)
    def _():
        pl.semaphore_signal(barrier, inc=1, device_id={"seq": me + 1}, device_id_type=MESH)

    def partner(level):
        bit = lax.rem(lax.div(me, 1 << level), 2)
        return me + (1 << level) * (1 - 2 * bit)

    for level in range(levels):
        pl.semaphore_signal(barrier, inc=1, device_id={"seq": partner(level)}, device_id_type=MESH)
    for load in loads:
        load.start()
    ends = has_left.astype(jnp.int32) + has_right.astype(jnp.int32)
    pl.semaphore_wait(barrier, levels + ends)

    def to_right():
        return pltpu.make_async_remote_copy(
            kv_hbm, halo.at[0], send_sem.at[0], recv_sem.at[0],
            device_id={"seq": me + 1}, device_id_type=MESH,
        )

    def to_left():
        return pltpu.make_async_remote_copy(
            kv_hbm, halo.at[1], send_sem.at[1], recv_sem.at[1],
            device_id={"seq": me - 1}, device_id_type=MESH,
        )

    @pl.when(has_right)
    def _():
        to_right().start()

    @pl.when(has_left)
    def _():
        to_left().start()

    wide = 2 * HEAD_SIZE
    ones = jnp.ones((rows, wide), jnp.bfloat16)
    zeros = jnp.zeros((rows, wide), jnp.bfloat16)

    loads[0].wait()
    spread(kv[:, :wide], kv[:, wide:], ones, kx, vx, 0)
    loads[1].wait()
    row = lax.broadcasted_iota(jnp.int32, (rows, rows), 0)
    col = lax.broadcasted_iota(jnp.int32, (rows, rows), 1)
    apart = jnp.abs(row - col)
    for pair in range(pairs):
        queries = q[:, pair * wide : (pair + 1) * wide]
        for odd in range(2):
            h = 2 * pair + odd
            scores = dot_nt(queries, kx[0, pair // per_group, odd])
            scores = jnp.where(apart <= extent[h], scores, HIDE)
            top = row_max([scores])
            tops[h] = jnp.broadcast_to(top, (rows, wide))
            accs[h] = dot(weight(scores, top), vx[0, pair // per_group, odd])

    @pl.when(has_left)
    def _():
        to_right().wait_recv()

    @pl.when(jnp.logical_not(has_left))
    def _():
        halo[0] = jnp.zeros(halo.shape[1:], jnp.bfloat16)

    @pl.when(has_right)
    def _():
        to_left().wait_recv()

    @pl.when(jnp.logical_not(has_right))
    def _():
        halo[1] = jnp.zeros(halo.shape[1:], jnp.bfloat16)

    for side in range(2):
        spread(halo[side, :, :wide], halo[side, :, wide:], ones, kx, vx, 1 + side)
    far = 4 * n * rows
    left_off = rows + jnp.where(has_left, 0, far)
    right_off = rows + jnp.where(has_right, 0, far)
    for tile in range(2):
        here = slice(tile * half, (tile + 1) * half)
        left = slice(0, rows) if tile == 0 else slice(half, rows)
        right = slice(0, half) if tile == 0 else slice(0, rows)
        left_apart = (row - col)[here, left] + left_off
        right_apart = (col - row)[here, right] + right_off
        for pair in range(pairs):
            queries = q[here, pair * wide : (pair + 1) * wide]
            group = pair // per_group
            done = []
            for odd in range(2):
                h = 2 * pair + odd
                a = dot_nt(queries, kx[1, group, odd, left])
                b = dot_nt(queries, kx[2, group, odd, right])
                a = jnp.where(left_apart <= extent[h], a, HIDE)
                b = jnp.where(right_apart <= extent[h], b, HIDE)
                before = tops[h, here, 0:1]
                top = jnp.maximum(before, row_max([a, b]))
                acc = accs[h, here] * jnp.exp(before - top)
                acc += dot(weight(a, top), vx[1, group, odd, left])
                acc += dot(weight(b, top), vx[2, group, odd, right])
                done.append(acc)
            att[here, pair * wide : (pair + 1) * wide] = joined(*done)

    loads[2].wait()
    loads[3].wait()
    hidden = (dot(att[...], wo1[...]) + res[...].astype(jnp.float32)).astype(jnp.bfloat16)
    hid[...] = hidden
    values = hidden.astype(jnp.float32)
    scale = lax.rsqrt(jnp.mean(values * values, axis=-1, keepdims=True) + 1e-05)
    normed = (values * scale).astype(jnp.bfloat16)
    loads[4].wait()
    kv2[...] = dot(normed, wkv2[...]).astype(jnp.bfloat16)
    swaps = [
        pltpu.make_async_remote_copy(
            kv2, kv2_in.at[level], send_sem.at[2 + level], recv_sem.at[2 + level],
            device_id={"seq": partner(level)}, device_id_type=MESH,
        )
        for level in range(levels)
    ]
    for swap in reversed(swaps):
        swap.start()
    loads[5].wait()
    q[...] = dot(normed, wq2[...]).astype(jnp.bfloat16)
    own = kv2[...]
    spread(own[:, :wide], own[:, wide:], ones, kx, vx, 0)

    chunks = [list(range(0, min(3, levels + 1)))]
    while chunks[-1][-1] < levels:
        first = chunks[-1][-1] + 1
        chunks.append(list(range(first, min(first + 2, levels + 1))))
    for chunk in chunks:
        for slot in chunk:
            if slot > 0:
                swaps[slot - 1].wait_recv()
                seen = mask[0, slot - 1] == 1
                spread(
                    jnp.where(seen, kv2_in[slot - 1, :, :wide], kv2[:, :wide]),
                    jnp.where(seen, kv2_in[slot - 1, :, wide:], zeros),
                    jnp.where(seen, ones, zeros),
                    kx, vx, slot,
                )
        for pair in range(pairs):
            queries = q[:, pair * wide : (pair + 1) * wide]
            group = pair // per_group
            done = []
            for odd in range(2):
                h = 2 * pair + odd
                parts = [dot_nt(queries, kx[slot, group, odd]) for slot in chunk]
                top = row_max(parts)
                acc = None
                if chunk[0] > 0:
                    before = tops[h, :, 0:1]
                    top = jnp.maximum(before, top)
                    acc = accs[h] * jnp.exp(before - top)
                for slot, part in zip(chunk, parts):
                    term = dot(weight(part, top), vx[slot, group, odd])
                    acc = term if acc is None else acc + term
                if chunk[-1] < levels:
                    tops[h] = jnp.broadcast_to(top, (rows, wide))
                    accs[h] = acc
                done.append(acc)
            if chunk[-1] == levels:
                att[:, pair * wide : (pair + 1) * wide] = joined(*done)

    loads[6].wait()
    stores = []
    for tile in range(2):
        here = slice(tile * half, (tile + 1) * half)
        out[here] = (dot(att[here], wo2[...]) + hid[here].astype(jnp.float32)).astype(jnp.bfloat16)
        stores.append(
            pltpu.make_async_copy(
                out.at[pl.ds(tile * half, half)],
                out_hbm.at[pl.ds(tile * half, half)],
                local_sem.at[7 + tile],
            )
        )
        stores[-1].start()
    for swap in swaps:
        swap.wait_send()

    @pl.when(has_right)
    def _():
        to_right().wait_send()

    @pl.when(has_left)
    def _():
        to_left().wait_send()

    for store in stores:
        store.wait()


def shards(
    n, residual, layer_queries, layer_keyvals, head_window_extent, block_mask,
    first_out, second_query, second_keyval, second_out,
):
    levels = n.bit_length() - 1
    rows, width = residual.shape
    query_width = layer_queries.shape[1]
    kv_width = layer_keyvals.shape[1]
    wide = 2 * HEAD_SIZE
    blocks = max(3, levels + 1)
    bf16, f32 = jnp.bfloat16, jnp.float32
    anywhere = pl.BlockSpec(memory_space=pl.ANY)
    scalars = pl.BlockSpec(memory_space=pltpu.SMEM)
    return pl.pallas_call(
        functools.partial(body, n, levels),
        name="two_layers",
        out_shape=jax.ShapeDtypeStruct((rows, width), bf16),
        in_specs=[anywhere] * 3 + [scalars] * 2 + [anywhere] * 4,
        out_specs=anywhere,
        scratch_shapes=[
            pltpu.VMEM((rows, query_width), bf16),
            pltpu.VMEM((rows, kv_width), bf16),
            pltpu.VMEM((2, rows, kv_width), bf16),
            pltpu.VMEM((rows, width), bf16),
            pltpu.VMEM(first_out.shape, bf16),
            pltpu.VMEM(second_query.shape, bf16),
            pltpu.VMEM(second_keyval.shape, bf16),
            pltpu.VMEM(second_out.shape, bf16),
            pltpu.VMEM((rows, kv_width), bf16),
            pltpu.VMEM((levels, rows, kv_width), bf16),
            pltpu.VMEM((blocks, 2, 2, rows, wide), bf16),
            pltpu.VMEM((blocks, 2, 2, rows, wide), bf16),
            pltpu.VMEM((QUERY_HEADS, rows, wide), f32),
            pltpu.VMEM((QUERY_HEADS, rows, wide), f32),
            pltpu.VMEM((rows, query_width), bf16),
            pltpu.VMEM((rows, width), bf16),
            pltpu.VMEM((rows, width), bf16),
            pltpu.SemaphoreType.DMA((9,)),
            pltpu.SemaphoreType.DMA((2 + levels,)),
            pltpu.SemaphoreType.DMA((2 + levels,)),
        ],
        compiler_params=pltpu.CompilerParams(collective_id=0, has_side_effects=True),
    )(
        layer_queries, layer_keyvals, residual, head_window_extent, block_mask,
        first_out, second_query, second_keyval, second_out,
    )


def solution(mesh):
    placed = (
        P(("groups", "seq"), None),
        P(("groups", "seq"), None),
        P(("groups", "seq"), None),
        P(),
        P("seq", None),
        P(),
        P(),
        P(),
        P(),
    )
    return jax.shard_map(
        functools.partial(shards, mesh.shape["seq"]),
        mesh=mesh, in_specs=placed, out_specs=P(("groups", "seq"), None), check_vma=False,
    )
```

```python
import functools

import jax
import jax.numpy as jnp
from jax import lax
from jax.experimental import pallas as pl
from jax.experimental.pallas import tpu as pltpu
from jax.sharding import PartitionSpec as P

QUERY_HEADS = 8
HEAD_SIZE = 64
MESH = pl.DeviceIdType.MESH
HIDE = -1e30
TOTALS = 16
NT = (((1,), (1,)), ((), ()))


def dot_nt(a, b):
    return lax.dot_general(a, b, NT, preferred_element_type=jnp.float32)


def dot(a, b):
    return jnp.dot(a, b, preferred_element_type=jnp.float32)


def rolled(x):
    return jnp.concatenate([x[:, HEAD_SIZE:], x[:, :HEAD_SIZE]], axis=1)


def spread(keys, values, ones, kx, vt, slot):
    low = lax.broadcasted_iota(jnp.int32, keys.shape, 1) < HEAD_SIZE
    none = jnp.zeros_like(keys)
    first, second = jnp.where(low, keys, none), jnp.where(low, none, keys)
    kx[slot, 0, 0] = first
    kx[slot, 0, 1] = rolled(first)
    kx[slot, 1, 0] = rolled(second)
    kx[slot, 1, 1] = second
    for group in range(2):
        vt[slot, group, :HEAD_SIZE] = values[group * HEAD_SIZE : (group + 1) * HEAD_SIZE]
        vt[slot, group, HEAD_SIZE:] = ones


def col_max(parts):
    top = jnp.max(parts[0], axis=0, keepdims=True)
    for part in parts[1:]:
        top = jnp.maximum(top, jnp.max(part, axis=0, keepdims=True))
    return top


def weight(scores, top):
    return jnp.exp((scores - top).astype(jnp.bfloat16))


def shared(acc):
    return acc[:HEAD_SIZE] * (1.0 / acc[HEAD_SIZE : HEAD_SIZE + 1])


def body(
    n, levels,
    q_hbm, kv_hbm, res_hbm, extent, mask, wo1_hbm, wq2_hbm, wkv2_hbm,
    att_out, hid_out,
    q, kv, halo, res, wo1, wq2, wkv2, kv2, kv2_in, kx, vt, tops, accs, att, hid,
    local_sem, send_sem, recv_sem,
):
    rows = q.shape[0]
    wide = 2 * HEAD_SIZE
    pairs = q.shape[1] // wide
    per_group = pairs // 2
    scaled = jnp.bfloat16(HEAD_SIZE ** (-0.5))
    me = lax.axis_index("seq")
    loads = [
        pltpu.make_async_copy(src, dst, local_sem.at[i])
        for i, (src, dst) in enumerate(
            (
                (kv_hbm, kv),
                (q_hbm, q),
                (wo1_hbm, wo1),
                (res_hbm, res),
                (wkv2_hbm, wkv2),
                (wq2_hbm, wq2),
            )
        )
    ]
    barrier = pltpu.get_barrier_semaphore()
    has_left, has_right = me > 0, me < n - 1

    @pl.when(has_left)
    def _():
        pl.semaphore_signal(barrier, inc=1, device_id={"seq": me - 1}, device_id_type=MESH)

    @pl.when(has_right)
    def _():
        pl.semaphore_signal(barrier, inc=1, device_id={"seq": me + 1}, device_id_type=MESH)

    def partner(level):
        bit = lax.rem(lax.div(me, 1 << level), 2)
        return me + (1 << level) * (1 - 2 * bit)

    for level in range(levels):
        pl.semaphore_signal(barrier, inc=1, device_id={"seq": partner(level)}, device_id_type=MESH)
    for load in loads:
        load.start()
    ends = has_left.astype(jnp.int32) + has_right.astype(jnp.int32)
    pl.semaphore_wait(barrier, levels + ends)

    def to_right():
        return pltpu.make_async_remote_copy(
            kv_hbm, halo.at[0], send_sem.at[0], recv_sem.at[0],
            device_id={"seq": me + 1}, device_id_type=MESH,
        )

    def to_left():
        return pltpu.make_async_remote_copy(
            kv_hbm, halo.at[1], send_sem.at[1], recv_sem.at[1],
            device_id={"seq": me - 1}, device_id_type=MESH,
        )

    @pl.when(has_right)
    def _():
        to_right().start()

    @pl.when(has_left)
    def _():
        to_left().start()

    ones = jnp.ones((TOTALS, rows), jnp.bfloat16)

    loads[0].wait()
    spread(kv[:, :wide] * scaled, kv[:, wide:].T, ones, kx, vt, 0)
    loads[1].wait()
    key = lax.broadcasted_iota(jnp.int32, (rows, rows), 0)
    query = lax.broadcasted_iota(jnp.int32, (rows, rows), 1)
    apart = jnp.abs(key - query)
    for pair in range(pairs):
        queries = q[:, pair * wide : (pair + 1) * wide]
        for odd in range(2):
            h = 2 * pair + odd
            scores = dot_nt(kx[0, pair // per_group, odd], queries)
            scores = jnp.where(apart <= extent[h], scores, HIDE)
            top = col_max([scores])
            tops[h] = jnp.broadcast_to(top, tops.shape[1:])
            accs[h] = dot(vt[0, pair // per_group], weight(scores, top))

    @pl.when(has_left)
    def _():
        to_right().wait_recv()

    @pl.when(jnp.logical_not(has_left))
    def _():
        halo[0] = jnp.zeros(halo.shape[1:], jnp.bfloat16)

    @pl.when(has_right)
    def _():
        to_left().wait_recv()

    @pl.when(jnp.logical_not(has_right))
    def _():
        halo[1] = jnp.zeros(halo.shape[1:], jnp.bfloat16)

    for side in range(2):
        spread(halo[side, :, :wide] * scaled, halo[side, :, wide:].T, ones, kx, vt, 1 + side)
    far = 4 * n * rows
    left_apart = query - key + rows + jnp.where(has_left, 0, far)
    right_apart = key - query + rows + jnp.where(has_right, 0, far)
    for pair in range(pairs):
        queries = q[:, pair * wide : (pair + 1) * wide]
        group = pair // per_group
        done = []
        for odd in range(2):
            h = 2 * pair + odd
            a = dot_nt(kx[1, group, odd], queries)
            b = dot_nt(kx[2, group, odd], queries)
            a = jnp.where(left_apart <= extent[h], a, HIDE)
            b = jnp.where(right_apart <= extent[h], b, HIDE)
            before = tops[h, 0:1]
            top = jnp.maximum(before, col_max([a, b]))
            acc = accs[h] * jnp.exp(before - top)
            acc += dot(vt[1, group], weight(a, top))
            acc += dot(vt[2, group], weight(b, top))
            done.append(shared(acc))
        att[:, pair * wide : (pair + 1) * wide] = jnp.concatenate(done, axis=0).astype(jnp.bfloat16).T

    loads[2].wait()
    loads[3].wait()
    hidden = (dot(att[...], wo1[...]) + res[...].astype(jnp.float32)).astype(jnp.bfloat16)
    hid[...] = hidden
    values = hidden.astype(jnp.float32)
    scale = lax.rsqrt(jnp.mean(values * values, axis=-1, keepdims=True) + 1e-05)
    normed = (values * scale).astype(jnp.bfloat16)
    loads[4].wait()
    keyvals = dot(normed, wkv2[...]).astype(jnp.bfloat16)
    kv2[:rows] = keyvals[:, :wide] * scaled
    turned = keyvals[:, wide:].T
    for part in range(rows // wide):
        kv2[rows + part * wide : rows + (part + 1) * wide] = turned[:, part * wide : (part + 1) * wide]
    swaps = [
        pltpu.make_async_remote_copy(
            kv2, kv2_in.at[level], send_sem.at[2 + level], recv_sem.at[2 + level],
            device_id={"seq": partner(level)}, device_id_type=MESH,
        )
        for level in range(levels)
    ]
    for swap in reversed(swaps):
        swap.start()
    keep_hidden = pltpu.make_async_copy(hid, hid_out, local_sem.at[6])
    keep_hidden.start()
    loads[5].wait()
    q[...] = dot(normed, wq2[...]).astype(jnp.bfloat16)
    spread(kv2[:rows], turned, ones, kx, vt, 0)

    chunks = [list(range(0, min(3, levels + 1)))]
    while chunks[-1][-1] < levels:
        first = chunks[-1][-1] + 1
        chunks.append(list(range(first, min(first + 2, levels + 1))))
    for chunk in chunks:
        for slot in chunk:
            if slot > 0:
                swaps[slot - 1].wait_recv()
                seen = mask[0, slot - 1] == 1
                came = jnp.concatenate(
                    [
                        kv2_in[slot - 1, rows + part * wide : rows + (part + 1) * wide]
                        for part in range(rows // wide)
                    ],
                    axis=1,
                )
                spread(
                    jnp.where(seen, kv2_in[slot - 1, :rows], kv2[:rows]),
                    jnp.where(seen, came, jnp.zeros_like(came)),
                    jnp.where(seen, ones, jnp.zeros_like(ones)),
                    kx, vt, slot,
                )
        for pair in range(pairs):
            queries = q[:, pair * wide : (pair + 1) * wide]
            group = pair // per_group
            done = []
            for odd in range(2):
                h = 2 * pair + odd
                parts = [dot_nt(kx[slot, group, odd], queries) for slot in chunk]
                top = col_max(parts)
                acc = None
                if chunk[0] > 0:
                    before = tops[h, 0:1]
                    top = jnp.maximum(before, top)
                    acc = accs[h] * jnp.exp(before - top)
                for slot, part in zip(chunk, parts):
                    term = dot(vt[slot, group], weight(part, top))
                    acc = term if acc is None else acc + term
                if chunk[-1] < levels:
                    tops[h] = jnp.broadcast_to(top, tops.shape[1:])
                    accs[h] = acc
                else:
                    done.append(shared(acc))
            if done:
                att[:, pair * wide : (pair + 1) * wide] = (
                    jnp.concatenate(done, axis=0).astype(jnp.bfloat16).T
                )

    keep_att = pltpu.make_async_copy(att, att_out, local_sem.at[7])
    keep_att.start()
    for swap in swaps:
        swap.wait_send()

    @pl.when(has_right)
    def _():
        to_right().wait_send()

    @pl.when(has_left)
    def _():
        to_left().wait_send()

    keep_hidden.wait()
    keep_att.wait()


def shards(
    n, residual, layer_queries, layer_keyvals, head_window_extent, block_mask,
    first_out, second_query, second_keyval, second_out,
):
    levels = n.bit_length() - 1
    rows, width = residual.shape
    query_width = layer_queries.shape[1]
    kv_width = layer_keyvals.shape[1]
    wide = 2 * HEAD_SIZE
    blocks = max(3, levels + 1)
    bf16, f32 = jnp.bfloat16, jnp.float32
    anywhere = pl.BlockSpec(memory_space=pl.ANY)
    stays = pl.BlockSpec(memory_space=pltpu.HBM)
    scalars = pl.BlockSpec(memory_space=pltpu.SMEM)
    att, hidden = pl.pallas_call(
        functools.partial(body, n, levels),
        name="two_layers",
        out_shape=(
            jax.ShapeDtypeStruct((rows, query_width), bf16),
            jax.ShapeDtypeStruct((rows, width), bf16),
        ),
        in_specs=[stays] * 3 + [scalars] * 2 + [stays] * 3,
        out_specs=(anywhere, anywhere),
        scratch_shapes=[
            pltpu.VMEM((rows, query_width), bf16),
            pltpu.VMEM((rows, kv_width), bf16),
            pltpu.VMEM((2, rows, kv_width), bf16),
            pltpu.VMEM((rows, width), bf16),
            pltpu.VMEM(first_out.shape, bf16),
            pltpu.VMEM(second_query.shape, bf16),
            pltpu.VMEM(second_keyval.shape, bf16),
            pltpu.VMEM((2 * rows, wide), bf16),
            pltpu.VMEM((levels, 2 * rows, wide), bf16),
            pltpu.VMEM((blocks, 2, 2, rows, wide), bf16),
            pltpu.VMEM((blocks, 2, HEAD_SIZE + TOTALS, rows), bf16),
            pltpu.VMEM((QUERY_HEADS, 8, rows), f32),
            pltpu.VMEM((QUERY_HEADS, HEAD_SIZE + TOTALS, rows), f32),
            pltpu.VMEM((rows, query_width), bf16),
            pltpu.VMEM((rows, width), bf16),
            pltpu.SemaphoreType.DMA((8,)),
            pltpu.SemaphoreType.DMA((2 + levels,)),
            pltpu.SemaphoreType.DMA((2 + levels,)),
        ],
        compiler_params=pltpu.CompilerParams(
            collective_id=0, has_side_effects=True
        ),
    )(
        layer_queries, layer_keyvals, residual, head_window_extent, block_mask,
        first_out, second_query, second_keyval,
    )
    output = jnp.dot(att, second_out, preferred_element_type=f32) + hidden.astype(f32)
    return output.astype(bf16)


def solution(mesh):
    placed = (
        P(("groups", "seq"), None),
        P(("groups", "seq"), None),
        P(("groups", "seq"), None),
        P(),
        P("seq", None),
        P(),
        P(),
        P(),
        P(),
    )
    return jax.shard_map(
        functools.partial(shards, mesh.shape["seq"]),
        mesh=mesh, in_specs=placed, out_specs=P(("groups", "seq"), None), check_vma=False,
    )
```

```python
import functools

import jax
import jax.numpy as jnp
from jax import lax
from jax.experimental import pallas as pl
from jax.experimental.pallas import tpu as pltpu
from jax.sharding import PartitionSpec as P

QUERY_HEADS = 8
HEAD_SIZE = 64
MESH = pl.DeviceIdType.MESH
HIDE = -1e30
TOTALS = 16
NT = (((1,), (1,)), ((), ()))


def dot_nt(a, b):
    return lax.dot_general(a, b, NT, preferred_element_type=jnp.float32)


def dot(a, b):
    return jnp.dot(a, b, preferred_element_type=jnp.float32)


def rolled(x):
    return jnp.concatenate([x[:, HEAD_SIZE:], x[:, :HEAD_SIZE]], axis=1)


def spread(keys, values, ones, kx, vt, slot):
    low = lax.broadcasted_iota(jnp.int32, keys.shape, 1) < HEAD_SIZE
    none = jnp.zeros_like(keys)
    first, second = jnp.where(low, keys, none), jnp.where(low, none, keys)
    kx[slot, 0, 0] = first
    kx[slot, 0, 1] = rolled(first)
    kx[slot, 1, 0] = rolled(second)
    kx[slot, 1, 1] = second
    for group in range(2):
        vt[slot, group, :HEAD_SIZE] = values[group * HEAD_SIZE : (group + 1) * HEAD_SIZE]
        vt[slot, group, HEAD_SIZE:] = ones


def col_max(parts):
    top = jnp.max(parts[0], axis=0, keepdims=True)
    for part in parts[1:]:
        top = jnp.maximum(top, jnp.max(part, axis=0, keepdims=True))
    return top


def weight(scores, top):
    return jnp.exp((scores - top).astype(jnp.bfloat16))


def staggered(steps, scores, weigh, finish):
    ready, weighed = {}, {}
    count = len(steps)
    for at in range(count + 2):
        if at < count:
            ready[at] = scores(steps[at])
        if 0 <= at - 1 < count:
            weighed[at - 1] = weigh(steps[at - 1], ready.pop(at - 1))
        if 0 <= at - 2 < count:
            finish(steps[at - 2], *weighed.pop(at - 2))


def shared(acc):
    return acc[:HEAD_SIZE] * (1.0 / acc[HEAD_SIZE : HEAD_SIZE + 1])


def body(
    n, levels,
    q_hbm, kv_hbm, res_hbm, extent, mask, wo1_hbm, wq2_hbm, wkv2_hbm,
    att_out, hid_out,
    q, kv, halo, res, wo1, wq2, wkv2, kv2, kv2_in, kx, vt, tops, accs, att, hid,
    local_sem, send_sem, recv_sem,
):
    rows = q.shape[0]
    wide = 2 * HEAD_SIZE
    pairs = q.shape[1] // wide
    per_group = pairs // 2
    scaled = jnp.bfloat16(HEAD_SIZE ** (-0.5))
    me = lax.axis_index("seq")
    loads = [
        pltpu.make_async_copy(src, dst, local_sem.at[i])
        for i, (src, dst) in enumerate(
            (
                (kv_hbm, kv),
                (q_hbm, q),
                (wo1_hbm, wo1),
                (res_hbm, res),
                (wkv2_hbm, wkv2),
                (wq2_hbm, wq2),
            )
        )
    ]
    barrier = pltpu.get_barrier_semaphore()
    has_left, has_right = me > 0, me < n - 1

    @pl.when(has_left)
    def _():
        pl.semaphore_signal(barrier, inc=1, device_id={"seq": me - 1}, device_id_type=MESH)

    @pl.when(has_right)
    def _():
        pl.semaphore_signal(barrier, inc=1, device_id={"seq": me + 1}, device_id_type=MESH)

    def partner(level):
        bit = lax.rem(lax.div(me, 1 << level), 2)
        return me + (1 << level) * (1 - 2 * bit)

    for level in range(levels):
        pl.semaphore_signal(barrier, inc=1, device_id={"seq": partner(level)}, device_id_type=MESH)
    for load in loads:
        load.start()
    ends = has_left.astype(jnp.int32) + has_right.astype(jnp.int32)
    pl.semaphore_wait(barrier, levels + ends)

    def to_right():
        return pltpu.make_async_remote_copy(
            kv_hbm, halo.at[0], send_sem.at[0], recv_sem.at[0],
            device_id={"seq": me + 1}, device_id_type=MESH,
        )

    def to_left():
        return pltpu.make_async_remote_copy(
            kv_hbm, halo.at[1], send_sem.at[1], recv_sem.at[1],
            device_id={"seq": me - 1}, device_id_type=MESH,
        )

    @pl.when(has_right)
    def _():
        to_right().start()

    @pl.when(has_left)
    def _():
        to_left().start()

    ones = jnp.ones((TOTALS, rows), jnp.bfloat16)

    loads[0].wait()
    spread(kv[:, :wide] * scaled, kv[:, wide:].T, ones, kx, vt, 0)
    loads[1].wait()
    key = lax.broadcasted_iota(jnp.int32, (rows, rows), 0)
    query = lax.broadcasted_iota(jnp.int32, (rows, rows), 1)
    apart = jnp.abs(key - query)
    heads = list(range(2 * pairs))

    def queries_of(h):
        pair = h // 2
        return q[:, pair * wide : (pair + 1) * wide]

    def put(h, share, halves):
        halves.append(share)
        if h % 2:
            both = jnp.concatenate(halves, axis=0).astype(jnp.bfloat16)
            att[:, h // 2 * wide : (h // 2 + 1) * wide] = both.T
            halves.clear()

    def own_scores(h):
        return dot_nt(kx[0, h // 2 // per_group, h % 2], queries_of(h))

    def own_weigh(h, scores):
        scores = jnp.where(apart <= extent[h], scores, HIDE)
        top = col_max([scores])
        tops[h] = jnp.broadcast_to(top, tops.shape[1:])
        return (weight(scores, top),)

    def own_finish(h, shares):
        accs[h] = dot(vt[0, h // 2 // per_group], shares)

    staggered(heads, own_scores, own_weigh, own_finish)

    @pl.when(has_left)
    def _():
        to_right().wait_recv()

    @pl.when(jnp.logical_not(has_left))
    def _():
        halo[0] = jnp.zeros(halo.shape[1:], jnp.bfloat16)

    @pl.when(has_right)
    def _():
        to_left().wait_recv()

    @pl.when(jnp.logical_not(has_right))
    def _():
        halo[1] = jnp.zeros(halo.shape[1:], jnp.bfloat16)

    for side in range(2):
        spread(halo[side, :, :wide] * scaled, halo[side, :, wide:].T, ones, kx, vt, 1 + side)
    far = 4 * n * rows
    left_apart = query - key + rows + jnp.where(has_left, 0, far)
    right_apart = key - query + rows + jnp.where(has_right, 0, far)
    halves = []

    def side_scores(h):
        return [dot_nt(kx[side, h // 2 // per_group, h % 2], queries_of(h)) for side in (1, 2)]

    def side_weigh(h, parts):
        a = jnp.where(left_apart <= extent[h], parts[0], HIDE)
        b = jnp.where(right_apart <= extent[h], parts[1], HIDE)
        before = tops[h, 0:1]
        top = jnp.maximum(before, col_max([a, b]))
        return jnp.exp(before - top), weight(a, top), weight(b, top)

    def side_finish(h, fade, a, b):
        acc = accs[h] * fade
        acc += dot(vt[1, h // 2 // per_group], a)
        acc += dot(vt[2, h // 2 // per_group], b)
        put(h, shared(acc), halves)

    staggered(heads, side_scores, side_weigh, side_finish)

    loads[2].wait()
    loads[3].wait()
    hidden = (dot(att[...], wo1[...]) + res[...].astype(jnp.float32)).astype(jnp.bfloat16)
    hid[...] = hidden
    values = hidden.astype(jnp.float32)
    scale = lax.rsqrt(jnp.mean(values * values, axis=-1, keepdims=True) + 1e-05)
    normed = (values * scale).astype(jnp.bfloat16)
    loads[4].wait()
    keyvals = dot(normed, wkv2[...]).astype(jnp.bfloat16)
    kv2[:rows] = keyvals[:, :wide] * scaled
    turned = keyvals[:, wide:].T
    for part in range(rows // wide):
        kv2[rows + part * wide : rows + (part + 1) * wide] = turned[:, part * wide : (part + 1) * wide]
    swaps = [
        pltpu.make_async_remote_copy(
            kv2, kv2_in.at[level], send_sem.at[2 + level], recv_sem.at[2 + level],
            device_id={"seq": partner(level)}, device_id_type=MESH,
        )
        for level in range(levels)
    ]
    for swap in reversed(swaps):
        swap.start()
    keep_hidden = pltpu.make_async_copy(hid, hid_out, local_sem.at[6])
    keep_hidden.start()
    loads[5].wait()
    q[...] = dot(normed, wq2[...]).astype(jnp.bfloat16)
    spread(kv2[:rows], turned, ones, kx, vt, 0)

    chunks = [list(range(0, min(3, levels + 1)))]
    while chunks[-1][-1] < levels:
        first = chunks[-1][-1] + 1
        chunks.append(list(range(first, min(first + 2, levels + 1))))
    for chunk in chunks:
        for slot in chunk:
            if slot > 0:
                swaps[slot - 1].wait_recv()
                seen = mask[0, slot - 1] == 1
                came = jnp.concatenate(
                    [
                        kv2_in[slot - 1, rows + part * wide : rows + (part + 1) * wide]
                        for part in range(rows // wide)
                    ],
                    axis=1,
                )
                spread(
                    jnp.where(seen, kv2_in[slot - 1, :rows], kv2[:rows]),
                    jnp.where(seen, came, jnp.zeros_like(came)),
                    jnp.where(seen, ones, jnp.zeros_like(ones)),
                    kx, vt, slot,
                )

        def far_scores(h):
            return [dot_nt(kx[slot, h // 2 // per_group, h % 2], queries_of(h)) for slot in chunk]

        def far_weigh(h, parts):
            top = col_max(parts)
            fade = None
            if chunk[0] > 0:
                before = tops[h, 0:1]
                top = jnp.maximum(before, top)
                fade = jnp.exp(before - top)
            if chunk[-1] < levels:
                tops[h] = jnp.broadcast_to(top, tops.shape[1:])
            return fade, [weight(part, top) for part in parts]

        def far_finish(h, fade, parts):
            acc = None if fade is None else accs[h] * fade
            for slot, part in zip(chunk, parts):
                term = dot(vt[slot, h // 2 // per_group], part)
                acc = term if acc is None else acc + term
            if chunk[-1] < levels:
                accs[h] = acc
            else:
                put(h, shared(acc), halves)

        staggered(heads, far_scores, far_weigh, far_finish)

    keep_att = pltpu.make_async_copy(att, att_out, local_sem.at[7])
    keep_att.start()
    for swap in swaps:
        swap.wait_send()

    @pl.when(has_right)
    def _():
        to_right().wait_send()

    @pl.when(has_left)
    def _():
        to_left().wait_send()

    keep_hidden.wait()
    keep_att.wait()


def shards(
    n, residual, layer_queries, layer_keyvals, head_window_extent, block_mask,
    first_out, second_query, second_keyval, second_out,
):
    levels = n.bit_length() - 1
    rows, width = residual.shape
    query_width = layer_queries.shape[1]
    kv_width = layer_keyvals.shape[1]
    wide = 2 * HEAD_SIZE
    blocks = max(3, levels + 1)
    bf16, f32 = jnp.bfloat16, jnp.float32
    anywhere = pl.BlockSpec(memory_space=pl.ANY)
    stays = pl.BlockSpec(memory_space=pltpu.HBM)
    scalars = pl.BlockSpec(memory_space=pltpu.SMEM)
    att, hidden = pl.pallas_call(
        functools.partial(body, n, levels),
        name="two_layers",
        out_shape=(
            jax.ShapeDtypeStruct((rows, query_width), bf16),
            jax.ShapeDtypeStruct((rows, width), bf16),
        ),
        in_specs=[stays] * 3 + [scalars] * 2 + [stays] * 3,
        out_specs=(anywhere, anywhere),
        scratch_shapes=[
            pltpu.VMEM((rows, query_width), bf16),
            pltpu.VMEM((rows, kv_width), bf16),
            pltpu.VMEM((2, rows, kv_width), bf16),
            pltpu.VMEM((rows, width), bf16),
            pltpu.VMEM(first_out.shape, bf16),
            pltpu.VMEM(second_query.shape, bf16),
            pltpu.VMEM(second_keyval.shape, bf16),
            pltpu.VMEM((2 * rows, wide), bf16),
            pltpu.VMEM((levels, 2 * rows, wide), bf16),
            pltpu.VMEM((blocks, 2, 2, rows, wide), bf16),
            pltpu.VMEM((blocks, 2, HEAD_SIZE + TOTALS, rows), bf16),
            pltpu.VMEM((QUERY_HEADS, 8, rows), f32),
            pltpu.VMEM((QUERY_HEADS, HEAD_SIZE + TOTALS, rows), f32),
            pltpu.VMEM((rows, query_width), bf16),
            pltpu.VMEM((rows, width), bf16),
            pltpu.SemaphoreType.DMA((8,)),
            pltpu.SemaphoreType.DMA((2 + levels,)),
            pltpu.SemaphoreType.DMA((2 + levels,)),
        ],
        compiler_params=pltpu.CompilerParams(
            collective_id=0, has_side_effects=True
        ),
    )(
        layer_queries, layer_keyvals, residual, head_window_extent, block_mask,
        first_out, second_query, second_keyval,
    )
    output = jnp.dot(att, second_out, preferred_element_type=f32) + hidden.astype(f32)
    return output.astype(bf16)


def solution(mesh):
    placed = (
        P(("groups", "seq"), None),
        P(("groups", "seq"), None),
        P(("groups", "seq"), None),
        P(),
        P("seq", None),
        P(),
        P(),
        P(),
        P(),
    )
    return jax.shard_map(
        functools.partial(shards, mesh.shape["seq"]),
        mesh=mesh, in_specs=placed, out_specs=P(("groups", "seq"), None), check_vma=False,
    )
```

```python
import functools

import jax
import jax.numpy as jnp
from jax import lax
from jax.experimental import pallas as pl
from jax.experimental.pallas import tpu as pltpu
from jax.sharding import PartitionSpec as P

QUERY_HEADS = 8
HEAD_SIZE = 64
MESH = pl.DeviceIdType.MESH
HIDE = -1e30
TOTALS = 16
NT = (((1,), (1,)), ((), ()))


def dot_nt(a, b):
    return lax.dot_general(a, b, NT, preferred_element_type=jnp.float32)


def dot(a, b):
    return jnp.dot(a, b, preferred_element_type=jnp.float32)


def rolled(x):
    return jnp.concatenate([x[:, HEAD_SIZE:], x[:, :HEAD_SIZE]], axis=1)


def spread(keys, values, ones, kx, vt, slot):
    low = lax.broadcasted_iota(jnp.int32, keys.shape, 1) < HEAD_SIZE
    none = jnp.zeros_like(keys)
    first, second = jnp.where(low, keys, none), jnp.where(low, none, keys)
    kx[slot, 0, 0] = first
    kx[slot, 0, 1] = rolled(first)
    kx[slot, 1, 0] = rolled(second)
    kx[slot, 1, 1] = second
    for group in range(2):
        vt[slot, group, :HEAD_SIZE] = values[group * HEAD_SIZE : (group + 1) * HEAD_SIZE]
        vt[slot, group, HEAD_SIZE:] = ones


def col_max(parts):
    top = jnp.max(parts[0], axis=0, keepdims=True)
    for part in parts[1:]:
        top = jnp.maximum(top, jnp.max(part, axis=0, keepdims=True))
    return top


def weight(scores, top):
    return jnp.exp((scores - top).astype(jnp.bfloat16))


def staggered(steps, scores, weigh, finish):
    ready, weighed = {}, {}
    count = len(steps)
    for at in range(count + 2):
        if at < count:
            ready[at] = scores(steps[at])
        if 0 <= at - 1 < count:
            weighed[at - 1] = weigh(steps[at - 1], ready.pop(at - 1))
        if 0 <= at - 2 < count:
            finish(steps[at - 2], *weighed.pop(at - 2))


def shared(acc):
    return acc[:HEAD_SIZE] * (1.0 / acc[HEAD_SIZE : HEAD_SIZE + 1])


def body(
    n, levels,
    q_hbm, kv_hbm, res_hbm, extent, mask, wo1_hbm, wq2_hbm, wkv2_hbm,
    att_out, hid_out,
    q, kv, halo, res, wo1, wq2, wkv2, kv2, kv2_in, kx, vt, tops, accs, att, hid,
    local_sem, send_sem, recv_sem,
):
    rows = q.shape[0]
    wide = 2 * HEAD_SIZE
    pairs = q.shape[1] // wide
    per_group = pairs // 2
    scaled = jnp.bfloat16(HEAD_SIZE ** (-0.5))
    me = lax.axis_index("seq")
    loads = [
        pltpu.make_async_copy(src, dst, local_sem.at[i])
        for i, (src, dst) in enumerate(
            (
                (kv_hbm, kv),
                (q_hbm, q),
                (wo1_hbm, wo1),
                (res_hbm, res),
                (wkv2_hbm, wkv2),
                (wq2_hbm, wq2),
            )
        )
    ]
    barrier = pltpu.get_barrier_semaphore()
    has_left, has_right = me > 0, me < n - 1

    @pl.when(has_left)
    def _():
        pl.semaphore_signal(barrier, inc=1, device_id={"seq": me - 1}, device_id_type=MESH)

    @pl.when(has_right)
    def _():
        pl.semaphore_signal(barrier, inc=1, device_id={"seq": me + 1}, device_id_type=MESH)

    def partner(level):
        bit = lax.rem(lax.div(me, 1 << level), 2)
        return me + (1 << level) * (1 - 2 * bit)

    for level in range(levels):
        pl.semaphore_signal(barrier, inc=1, device_id={"seq": partner(level)}, device_id_type=MESH)
    for load in loads:
        load.start()
    ends = has_left.astype(jnp.int32) + has_right.astype(jnp.int32)
    pl.semaphore_wait(barrier, levels + ends)

    def to_right():
        return pltpu.make_async_remote_copy(
            kv_hbm, halo.at[0], send_sem.at[0], recv_sem.at[0],
            device_id={"seq": me + 1}, device_id_type=MESH,
        )

    def to_left():
        return pltpu.make_async_remote_copy(
            kv_hbm, halo.at[1], send_sem.at[1], recv_sem.at[1],
            device_id={"seq": me - 1}, device_id_type=MESH,
        )

    @pl.when(has_right)
    def _():
        to_right().start()

    @pl.when(has_left)
    def _():
        to_left().start()

    ones = jnp.ones((TOTALS, rows), jnp.bfloat16)

    loads[0].wait()
    spread(kv[:, :wide] * scaled, kv[:, wide:].T, ones, kx, vt, 0)
    loads[1].wait()
    key = lax.broadcasted_iota(jnp.int32, (rows, rows), 0)
    query = lax.broadcasted_iota(jnp.int32, (rows, rows), 1)
    apart = jnp.abs(key - query)
    heads = list(range(2 * pairs))

    def queries_of(h):
        pair = h // 2
        return q[:, pair * wide : (pair + 1) * wide]

    def put(h, share, halves):
        halves.append(share)
        if h % 2:
            both = jnp.concatenate(halves, axis=0).astype(jnp.bfloat16)
            att[:, h // 2 * wide : (h // 2 + 1) * wide] = both.T
            halves.clear()

    def own_scores(h):
        return dot_nt(kx[0, h // 2 // per_group, h % 2], queries_of(h))

    def own_weigh(h, scores):
        scores = jnp.where(apart <= extent[h], scores, HIDE)
        top = col_max([scores])
        tops[h] = jnp.broadcast_to(top, tops.shape[1:])
        return (weight(scores, top),)

    def own_finish(h, shares):
        accs[h] = dot(vt[0, h // 2 // per_group], shares)

    staggered(heads, own_scores, own_weigh, own_finish)

    @pl.when(has_left)
    def _():
        to_right().wait_recv()

    @pl.when(jnp.logical_not(has_left))
    def _():
        halo[0] = jnp.zeros(halo.shape[1:], jnp.bfloat16)

    @pl.when(has_right)
    def _():
        to_left().wait_recv()

    @pl.when(jnp.logical_not(has_right))
    def _():
        halo[1] = jnp.zeros(halo.shape[1:], jnp.bfloat16)

    for side in range(2):
        spread(halo[side, :, :wide] * scaled, halo[side, :, wide:].T, ones, kx, vt, 1 + side)
    far = 4 * n * rows
    left_apart = query - key + rows + jnp.where(has_left, 0, far)
    right_apart = key - query + rows + jnp.where(has_right, 0, far)
    halves = []

    def side_scores(h):
        return [dot_nt(kx[side, h // 2 // per_group, h % 2], queries_of(h)) for side in (1, 2)]

    def side_weigh(h, parts):
        a = jnp.where(left_apart <= extent[h], parts[0], HIDE)
        b = jnp.where(right_apart <= extent[h], parts[1], HIDE)
        before = tops[h, 0:1]
        top = jnp.maximum(before, col_max([a, b]))
        return jnp.exp(before - top), weight(a, top), weight(b, top)

    def side_finish(h, fade, a, b):
        acc = accs[h] * fade
        acc += dot(vt[1, h // 2 // per_group], a)
        acc += dot(vt[2, h // 2 // per_group], b)
        put(h, shared(acc), halves)

    staggered(heads, side_scores, side_weigh, side_finish)

    loads[2].wait()
    loads[3].wait()
    hidden = (dot(att[...], wo1[...]) + res[...].astype(jnp.float32)).astype(jnp.bfloat16)
    hid[...] = hidden
    values = hidden.astype(jnp.float32)
    scale = lax.rsqrt(jnp.mean(values * values, axis=-1, keepdims=True) + 1e-05)
    normed = (values * scale).astype(jnp.bfloat16)
    loads[4].wait()
    keyvals = dot(normed, wkv2[...]).astype(jnp.bfloat16)
    kv2[:rows] = keyvals[:, :wide] * scaled
    turned = keyvals[:, wide:].T
    for part in range(rows // wide):
        kv2[rows + part * wide : rows + (part + 1) * wide] = turned[:, part * wide : (part + 1) * wide]
    swaps = [
        pltpu.make_async_remote_copy(
            kv2, kv2_in.at[level], send_sem.at[2 + level], recv_sem.at[2 + level],
            device_id={"seq": partner(level)}, device_id_type=MESH,
        )
        for level in range(levels)
    ]
    for swap in swaps:
        swap.start()
    keep_hidden = pltpu.make_async_copy(hid, hid_out, local_sem.at[6])
    keep_hidden.start()
    loads[5].wait()
    q[...] = dot(normed, wq2[...]).astype(jnp.bfloat16)
    spread(kv2[:rows], turned, ones, kx, vt, 0)

    chunks, first = [], 0
    while first <= levels:
        size = 2 if first + 1 < levels else 1
        chunks.append(list(range(first, first + size)))
        first += size
    for chunk in chunks:
        for slot in chunk:
            if slot > 0:
                swaps[slot - 1].wait_recv()
                seen = mask[0, slot - 1] == 1
                came = jnp.concatenate(
                    [
                        kv2_in[slot - 1, rows + part * wide : rows + (part + 1) * wide]
                        for part in range(rows // wide)
                    ],
                    axis=1,
                )
                spread(
                    jnp.where(seen, kv2_in[slot - 1, :rows], kv2[:rows]),
                    jnp.where(seen, came, jnp.zeros_like(came)),
                    jnp.where(seen, ones, jnp.zeros_like(ones)),
                    kx, vt, slot,
                )

        def far_scores(h):
            return [dot_nt(kx[slot, h // 2 // per_group, h % 2], queries_of(h)) for slot in chunk]

        def far_weigh(h, parts):
            top = col_max(parts)
            fade = None
            if chunk[0] > 0:
                before = tops[h, 0:1]
                top = jnp.maximum(before, top)
                fade = jnp.exp(before - top)
            if chunk[-1] < levels:
                tops[h] = jnp.broadcast_to(top, tops.shape[1:])
            return fade, [weight(part, top) for part in parts]

        def far_finish(h, fade, parts):
            acc = None if fade is None else accs[h] * fade
            for slot, part in zip(chunk, parts):
                term = dot(vt[slot, h // 2 // per_group], part)
                acc = term if acc is None else acc + term
            if chunk[-1] < levels:
                accs[h] = acc
            else:
                put(h, shared(acc), halves)

        staggered(heads, far_scores, far_weigh, far_finish)

    keep_att = pltpu.make_async_copy(att, att_out, local_sem.at[7])
    keep_att.start()
    for swap in swaps:
        swap.wait_send()

    @pl.when(has_right)
    def _():
        to_right().wait_send()

    @pl.when(has_left)
    def _():
        to_left().wait_send()

    keep_hidden.wait()
    keep_att.wait()


def shards(
    n, residual, layer_queries, layer_keyvals, head_window_extent, block_mask,
    first_out, second_query, second_keyval, second_out,
):
    levels = n.bit_length() - 1
    rows, width = residual.shape
    query_width = layer_queries.shape[1]
    kv_width = layer_keyvals.shape[1]
    wide = 2 * HEAD_SIZE
    blocks = max(3, levels + 1)
    bf16, f32 = jnp.bfloat16, jnp.float32
    anywhere = pl.BlockSpec(memory_space=pl.ANY)
    stays = pl.BlockSpec(memory_space=pltpu.HBM)
    scalars = pl.BlockSpec(memory_space=pltpu.SMEM)
    att, hidden = pl.pallas_call(
        functools.partial(body, n, levels),
        name="two_layers",
        out_shape=(
            jax.ShapeDtypeStruct((rows, query_width), bf16),
            jax.ShapeDtypeStruct((rows, width), bf16),
        ),
        in_specs=[stays] * 3 + [scalars] * 2 + [stays] * 3,
        out_specs=(anywhere, anywhere),
        scratch_shapes=[
            pltpu.VMEM((rows, query_width), bf16),
            pltpu.VMEM((rows, kv_width), bf16),
            pltpu.VMEM((2, rows, kv_width), bf16),
            pltpu.VMEM((rows, width), bf16),
            pltpu.VMEM(first_out.shape, bf16),
            pltpu.VMEM(second_query.shape, bf16),
            pltpu.VMEM(second_keyval.shape, bf16),
            pltpu.VMEM((2 * rows, wide), bf16),
            pltpu.VMEM((levels, 2 * rows, wide), bf16),
            pltpu.VMEM((blocks, 2, 2, rows, wide), bf16),
            pltpu.VMEM((blocks, 2, HEAD_SIZE + TOTALS, rows), bf16),
            pltpu.VMEM((QUERY_HEADS, 8, rows), f32),
            pltpu.VMEM((QUERY_HEADS, HEAD_SIZE + TOTALS, rows), f32),
            pltpu.VMEM((rows, query_width), bf16),
            pltpu.VMEM((rows, width), bf16),
            pltpu.SemaphoreType.DMA((8,)),
            pltpu.SemaphoreType.DMA((2 + levels,)),
            pltpu.SemaphoreType.DMA((2 + levels,)),
        ],
        compiler_params=pltpu.CompilerParams(
            collective_id=0, has_side_effects=True
        ),
    )(
        layer_queries, layer_keyvals, residual, head_window_extent, block_mask,
        first_out, second_query, second_keyval,
    )
    output = jnp.dot(att, second_out, preferred_element_type=f32) + hidden.astype(f32)
    return output.astype(bf16)


def solution(mesh):
    placed = (
        P(("groups", "seq"), None),
        P(("groups", "seq"), None),
        P(("groups", "seq"), None),
        P(),
        P("seq", None),
        P(),
        P(),
        P(),
        P(),
    )
    return jax.shard_map(
        functools.partial(shards, mesh.shape["seq"]),
        mesh=mesh, in_specs=placed, out_specs=P(("groups", "seq"), None), check_vma=False,
    )
```

```python
import functools

import jax
import jax.numpy as jnp
from jax import lax
from jax.experimental import pallas as pl
from jax.experimental.pallas import tpu as pltpu
from jax.sharding import PartitionSpec as P

QUERY_HEADS = 8
HEAD_SIZE = 64
MESH = pl.DeviceIdType.MESH
HIDE = -1e30
TOTALS = 16
NT = (((1,), (1,)), ((), ()))


def dot_nt(a, b):
    return lax.dot_general(a, b, NT, preferred_element_type=jnp.float32)


def dot(a, b):
    return jnp.dot(a, b, preferred_element_type=jnp.float32)


def rolled(x):
    return jnp.concatenate([x[:, HEAD_SIZE:], x[:, :HEAD_SIZE]], axis=1)


def spread(keys, values, ones, kx, vt, slot):
    low = lax.broadcasted_iota(jnp.int32, keys.shape, 1) < HEAD_SIZE
    none = jnp.zeros_like(keys)
    first, second = jnp.where(low, keys, none), jnp.where(low, none, keys)
    kx[slot, 0, 0] = first
    kx[slot, 0, 1] = rolled(first)
    kx[slot, 1, 0] = rolled(second)
    kx[slot, 1, 1] = second
    for group in range(2):
        vt[slot, group, :HEAD_SIZE] = values[group * HEAD_SIZE : (group + 1) * HEAD_SIZE]
        vt[slot, group, HEAD_SIZE:] = ones


def col_max(parts):
    top = jnp.max(parts[0], axis=0, keepdims=True)
    for part in parts[1:]:
        top = jnp.maximum(top, jnp.max(part, axis=0, keepdims=True))
    return top


def weight(scores, top):
    return jnp.exp((scores - top).astype(jnp.bfloat16))


def staggered(steps, scores, weigh, finish):
    ready, weighed = {}, {}
    count = len(steps)
    for at in range(count + 2):
        if at < count:
            ready[at] = scores(steps[at])
        if 0 <= at - 1 < count:
            weighed[at - 1] = weigh(steps[at - 1], ready.pop(at - 1))
        if 0 <= at - 2 < count:
            finish(steps[at - 2], *weighed.pop(at - 2))


def shared(acc):
    return acc[:HEAD_SIZE] * (1.0 / acc[HEAD_SIZE : HEAD_SIZE + 1])


def body(
    n, levels,
    q_hbm, kv_hbm, res_hbm, extent, mask, wo1_hbm, wq2_hbm, wkv2_hbm,
    att_out, hid_out,
    q, kv, halo, res, wo1, wq2, wkv2, kv2, kv2_in, kx, vt, tops, accs, att, hid,
    local_sem, send_sem, recv_sem,
):
    rows = q.shape[0]
    wide = 2 * HEAD_SIZE
    pairs = q.shape[1] // wide
    per_group = pairs // 2
    scaled = jnp.bfloat16(HEAD_SIZE ** (-0.5))
    me = lax.axis_index("seq")
    loads = [
        pltpu.make_async_copy(src, dst, local_sem.at[i])
        for i, (src, dst) in enumerate(
            (
                (kv_hbm, kv),
                (q_hbm, q),
                (wo1_hbm, wo1),
                (res_hbm, res),
                (wkv2_hbm, wkv2),
                (wq2_hbm, wq2),
            )
        )
    ]
    barrier = pltpu.get_barrier_semaphore()
    has_left, has_right = me > 0, me < n - 1

    @pl.when(has_left)
    def _():
        pl.semaphore_signal(barrier, inc=1, device_id={"seq": me - 1}, device_id_type=MESH)

    @pl.when(has_right)
    def _():
        pl.semaphore_signal(barrier, inc=1, device_id={"seq": me + 1}, device_id_type=MESH)

    def partner(level):
        bit = lax.rem(lax.div(me, 1 << level), 2)
        return me + (1 << level) * (1 - 2 * bit)

    for level in range(levels):
        pl.semaphore_signal(barrier, inc=1, device_id={"seq": partner(level)}, device_id_type=MESH)
    for load in loads:
        load.start()
    ends = has_left.astype(jnp.int32) + has_right.astype(jnp.int32)
    pl.semaphore_wait(barrier, levels + ends)

    def to_right():
        return pltpu.make_async_remote_copy(
            kv_hbm, halo.at[0], send_sem.at[0], recv_sem.at[0],
            device_id={"seq": me + 1}, device_id_type=MESH,
        )

    def to_left():
        return pltpu.make_async_remote_copy(
            kv_hbm, halo.at[1], send_sem.at[1], recv_sem.at[1],
            device_id={"seq": me - 1}, device_id_type=MESH,
        )

    @pl.when(has_right)
    def _():
        to_right().start()

    @pl.when(has_left)
    def _():
        to_left().start()

    ones = jnp.ones((TOTALS, rows), jnp.bfloat16)

    loads[0].wait()
    spread(kv[:, :wide] * scaled, kv[:, wide:].T, ones, kx, vt, 0)
    loads[1].wait()
    key = lax.broadcasted_iota(jnp.int32, (rows, rows), 0)
    query = lax.broadcasted_iota(jnp.int32, (rows, rows), 1)
    apart = jnp.abs(key - query)
    heads = list(range(2 * pairs))

    def queries_of(h):
        pair = h // 2
        return q[:, pair * wide : (pair + 1) * wide]

    def put(h, share, halves, here):
        halves.append(share)
        if h % 2:
            both = jnp.concatenate(halves, axis=0).astype(jnp.bfloat16)
            att[here, h // 2 * wide : (h // 2 + 1) * wide] = both.T
            halves.clear()

    def own_scores(h):
        return dot_nt(kx[0, h // 2 // per_group, h % 2], queries_of(h))

    def own_weigh(h, scores):
        scores = jnp.where(apart <= extent[h], scores, HIDE)
        top = col_max([scores])
        tops[h] = jnp.broadcast_to(top, tops.shape[1:])
        return (weight(scores, top),)

    def own_finish(h, shares):
        accs[h] = dot(vt[0, h // 2 // per_group], shares)

    staggered(heads, own_scores, own_weigh, own_finish)

    @pl.when(has_left)
    def _():
        to_right().wait_recv()

    @pl.when(jnp.logical_not(has_left))
    def _():
        halo[0] = jnp.zeros(halo.shape[1:], jnp.bfloat16)

    @pl.when(has_right)
    def _():
        to_left().wait_recv()

    @pl.when(jnp.logical_not(has_right))
    def _():
        halo[1] = jnp.zeros(halo.shape[1:], jnp.bfloat16)

    for side in range(2):
        spread(halo[side, :, :wide] * scaled, halo[side, :, wide:].T, ones, kx, vt, 1 + side)
    far = 4 * n * rows
    left_off = rows + jnp.where(has_left, 0, far)
    right_off = rows + jnp.where(has_right, 0, far)
    tiles = rows // wide
    for i in (2, 3, 4):
        loads[i].wait()
    swaps = [
        [
            pltpu.make_async_remote_copy(
                kv2.at[pl.ds(tile * 2 * wide, 2 * wide)],
                kv2_in.at[level, pl.ds(tile * 2 * wide, 2 * wide)],
                send_sem.at[2 + level * tiles + tile],
                recv_sem.at[2 + level * tiles + tile],
                device_id={"seq": partner(level)}, device_id_type=MESH,
            )
            for tile in range(tiles)
        ]
        for level in range(levels)
    ]
    halves, normed, turned = [], [], []
    for tile in range(tiles):
        here = slice(tile * wide, (tile + 1) * wide)
        left = slice(tile * wide, rows)
        right = slice(0, (tile + 1) * wide)
        left_apart = (query - key)[left, here] + left_off
        right_apart = (key - query)[right, here] + right_off

        def side_scores(h):
            pair = h // 2
            queries = q[here, pair * wide : (pair + 1) * wide]
            return [
                dot_nt(kx[1, pair // per_group, h % 2, left], queries),
                dot_nt(kx[2, pair // per_group, h % 2, right], queries),
            ]

        def side_weigh(h, parts):
            a = jnp.where(left_apart <= extent[h], parts[0], HIDE)
            b = jnp.where(right_apart <= extent[h], parts[1], HIDE)
            before = tops[h, 0:1, here]
            top = jnp.maximum(before, col_max([a, b]))
            return jnp.exp(before - top), weight(a, top), weight(b, top)

        def side_finish(h, fade, a, b):
            acc = accs[h, :, here] * fade
            acc += dot(vt[1, h // 2 // per_group, :, left], a)
            acc += dot(vt[2, h // 2 // per_group, :, right], b)
            put(h, shared(acc), halves, here)

        staggered(heads, side_scores, side_weigh, side_finish)

        hidden = (dot(att[here], wo1[...]) + res[here].astype(jnp.float32)).astype(jnp.bfloat16)
        hid[here] = hidden
        values = hidden.astype(jnp.float32)
        scale = lax.rsqrt(jnp.mean(values * values, axis=-1, keepdims=True) + 1e-05)
        normed.append((values * scale).astype(jnp.bfloat16))
        keyvals = dot(normed[-1], wkv2[...]).astype(jnp.bfloat16)
        turned.append(keyvals[:, wide:].T)
        kv2[tile * 2 * wide : (tile * 2 + 1) * wide] = keyvals[:, :wide] * scaled
        kv2[(tile * 2 + 1) * wide : (tile * 2 + 2) * wide] = turned[-1]
        for swap in swaps:
            swap[tile].start()

    def keys_of(block):
        return jnp.concatenate([block[2 * t * wide : (2 * t + 1) * wide] for t in range(tiles)], axis=0)

    def values_of(block):
        return jnp.concatenate(
            [block[(2 * t + 1) * wide : (2 * t + 2) * wide] for t in range(tiles)], axis=1
        )

    keep_hidden = pltpu.make_async_copy(hid, hid_out, local_sem.at[6])
    keep_hidden.start()
    loads[5].wait()
    q[...] = dot(jnp.concatenate(normed, axis=0), wq2[...]).astype(jnp.bfloat16)
    spread(keys_of(kv2), values_of(kv2), ones, kx, vt, 0)

    chunks, first = [], 0
    while first <= levels:
        size = 2 if first + 1 < levels else 1
        chunks.append(list(range(first, first + size)))
        first += size
    for chunk in chunks:
        for slot in chunk:
            if slot > 0:
                for swap in swaps[slot - 1]:
                    swap.wait_recv()
                seen = mask[0, slot - 1] == 1
                came = values_of(kv2_in[slot - 1])
                spread(
                    jnp.where(seen, keys_of(kv2_in[slot - 1]), keys_of(kv2)),
                    jnp.where(seen, came, jnp.zeros_like(came)),
                    jnp.where(seen, ones, jnp.zeros_like(ones)),
                    kx, vt, slot,
                )

        def far_scores(h):
            return [dot_nt(kx[slot, h // 2 // per_group, h % 2], queries_of(h)) for slot in chunk]

        def far_weigh(h, parts):
            top = col_max(parts)
            fade = None
            if chunk[0] > 0:
                before = tops[h, 0:1]
                top = jnp.maximum(before, top)
                fade = jnp.exp(before - top)
            if chunk[-1] < levels:
                tops[h] = jnp.broadcast_to(top, tops.shape[1:])
            return fade, [weight(part, top) for part in parts]

        def far_finish(h, fade, parts):
            acc = None if fade is None else accs[h] * fade
            for slot, part in zip(chunk, parts):
                term = dot(vt[slot, h // 2 // per_group], part)
                acc = term if acc is None else acc + term
            if chunk[-1] < levels:
                accs[h] = acc
            else:
                put(h, shared(acc), halves, slice(0, rows))

        staggered(heads, far_scores, far_weigh, far_finish)

    keep_att = pltpu.make_async_copy(att, att_out, local_sem.at[7])
    keep_att.start()
    for level in swaps:
        for swap in level:
            swap.wait_send()

    @pl.when(has_right)
    def _():
        to_right().wait_send()

    @pl.when(has_left)
    def _():
        to_left().wait_send()

    keep_hidden.wait()
    keep_att.wait()


def shards(
    n, residual, layer_queries, layer_keyvals, head_window_extent, block_mask,
    first_out, second_query, second_keyval, second_out,
):
    levels = n.bit_length() - 1
    rows, width = residual.shape
    query_width = layer_queries.shape[1]
    kv_width = layer_keyvals.shape[1]
    wide = 2 * HEAD_SIZE
    blocks = max(3, levels + 1)
    bf16, f32 = jnp.bfloat16, jnp.float32
    anywhere = pl.BlockSpec(memory_space=pl.ANY)
    stays = pl.BlockSpec(memory_space=pltpu.HBM)
    scalars = pl.BlockSpec(memory_space=pltpu.SMEM)
    att, hidden = pl.pallas_call(
        functools.partial(body, n, levels),
        name="two_layers",
        out_shape=(
            jax.ShapeDtypeStruct((rows, query_width), bf16),
            jax.ShapeDtypeStruct((rows, width), bf16),
        ),
        in_specs=[stays] * 3 + [scalars] * 2 + [stays] * 3,
        out_specs=(anywhere, anywhere),
        scratch_shapes=[
            pltpu.VMEM((rows, query_width), bf16),
            pltpu.VMEM((rows, kv_width), bf16),
            pltpu.VMEM((2, rows, kv_width), bf16),
            pltpu.VMEM((rows, width), bf16),
            pltpu.VMEM(first_out.shape, bf16),
            pltpu.VMEM(second_query.shape, bf16),
            pltpu.VMEM(second_keyval.shape, bf16),
            pltpu.VMEM((2 * rows, wide), bf16),
            pltpu.VMEM((levels, 2 * rows, wide), bf16),
            pltpu.VMEM((blocks, 2, 2, rows, wide), bf16),
            pltpu.VMEM((blocks, 2, HEAD_SIZE + TOTALS, rows), bf16),
            pltpu.VMEM((QUERY_HEADS, 8, rows), f32),
            pltpu.VMEM((QUERY_HEADS, HEAD_SIZE + TOTALS, rows), f32),
            pltpu.VMEM((rows, query_width), bf16),
            pltpu.VMEM((rows, width), bf16),
            pltpu.SemaphoreType.DMA((8,)),
            pltpu.SemaphoreType.DMA((2 + levels * (rows // wide),)),
            pltpu.SemaphoreType.DMA((2 + levels * (rows // wide),)),
        ],
        compiler_params=pltpu.CompilerParams(
            collective_id=0, has_side_effects=True
        ),
    )(
        layer_queries, layer_keyvals, residual, head_window_extent, block_mask,
        first_out, second_query, second_keyval,
    )
    output = jnp.dot(att, second_out, preferred_element_type=f32) + hidden.astype(f32)
    return output.astype(bf16)


def solution(mesh):
    placed = (
        P(("groups", "seq"), None),
        P(("groups", "seq"), None),
        P(("groups", "seq"), None),
        P(),
        P("seq", None),
        P(),
        P(),
        P(),
        P(),
    )
    return jax.shard_map(
        functools.partial(shards, mesh.shape["seq"]),
        mesh=mesh, in_specs=placed, out_specs=P(("groups", "seq"), None), check_vma=False,
    )
```

```python
import functools

import jax
import jax.numpy as jnp
from jax import lax
from jax.experimental import pallas as pl
from jax.experimental.pallas import tpu as pltpu
from jax.sharding import PartitionSpec as P

QUERY_HEADS = 8
HEAD_SIZE = 64
MESH = pl.DeviceIdType.MESH
HIDE = -1e30
TOTALS = 16
NT = (((1,), (1,)), ((), ()))


def dot_nt(a, b):
    return lax.dot_general(a, b, NT, preferred_element_type=jnp.float32)


def dot(a, b):
    return jnp.dot(a, b, preferred_element_type=jnp.float32)


def rolled(x):
    return jnp.concatenate([x[:, HEAD_SIZE:], x[:, :HEAD_SIZE]], axis=1)


def spread(keys, values, ones, kx, vt, slot, part=slice(None)):
    low = lax.broadcasted_iota(jnp.int32, keys.shape, 1) < HEAD_SIZE
    none = jnp.zeros_like(keys)
    first, second = jnp.where(low, keys, none), jnp.where(low, none, keys)
    kx[slot, 0, 0, part] = first
    kx[slot, 0, 1, part] = rolled(first)
    kx[slot, 1, 0, part] = rolled(second)
    kx[slot, 1, 1, part] = second
    for group in range(2):
        vt[slot, group, :HEAD_SIZE, part] = values[group * HEAD_SIZE : (group + 1) * HEAD_SIZE]
        vt[slot, group, HEAD_SIZE:, part] = ones


def col_max(parts):
    top = jnp.max(parts[0], axis=0, keepdims=True)
    for part in parts[1:]:
        top = jnp.maximum(top, jnp.max(part, axis=0, keepdims=True))
    return top


def weight(scores, top):
    return jnp.exp((scores - top).astype(jnp.bfloat16))


def staggered(steps, scores, weigh, finish):
    ready, weighed = {}, {}
    count = len(steps)
    for at in range(count + 2):
        if at < count:
            ready[at] = scores(steps[at])
        if 0 <= at - 1 < count:
            weighed[at - 1] = weigh(steps[at - 1], ready.pop(at - 1))
        if 0 <= at - 2 < count:
            finish(steps[at - 2], *weighed.pop(at - 2))


def shared(acc):
    return acc[:HEAD_SIZE] * (1.0 / acc[HEAD_SIZE : HEAD_SIZE + 1])


def body(
    n, levels,
    q_hbm, kv_hbm, res_hbm, extent, mask, wo1_hbm, wq2_hbm, wkv2_hbm,
    att_out, hid_out,
    q, kv, halo, res, wo1, wq2, wkv2, kv2, kv2_in, kx, vt, tops, accs, att, hid,
    local_sem, send_sem, recv_sem,
):
    rows = q.shape[0]
    wide = 2 * HEAD_SIZE
    pairs = q.shape[1] // wide
    per_group = pairs // 2
    scaled = jnp.bfloat16(HEAD_SIZE ** (-0.5))
    me = lax.axis_index("seq")
    loads = [
        pltpu.make_async_copy(src, dst, local_sem.at[i])
        for i, (src, dst) in enumerate(
            (
                (kv_hbm, kv),
                (q_hbm, q),
                (wo1_hbm, wo1),
                (res_hbm, res),
                (wkv2_hbm, wkv2),
                (wq2_hbm, wq2),
            )
        )
    ]
    barrier = pltpu.get_barrier_semaphore()
    has_left, has_right = me > 0, me < n - 1

    @pl.when(has_left)
    def _():
        pl.semaphore_signal(barrier, inc=1, device_id={"seq": me - 1}, device_id_type=MESH)

    @pl.when(has_right)
    def _():
        pl.semaphore_signal(barrier, inc=1, device_id={"seq": me + 1}, device_id_type=MESH)

    def partner(level):
        bit = lax.rem(lax.div(me, 1 << level), 2)
        return me + (1 << level) * (1 - 2 * bit)

    for level in range(levels):
        pl.semaphore_signal(barrier, inc=1, device_id={"seq": partner(level)}, device_id_type=MESH)
    for load in loads:
        load.start()
    ends = has_left.astype(jnp.int32) + has_right.astype(jnp.int32)
    pl.semaphore_wait(barrier, levels + ends)

    def to_right():
        return pltpu.make_async_remote_copy(
            kv_hbm, halo.at[0], send_sem.at[0], recv_sem.at[0],
            device_id={"seq": me + 1}, device_id_type=MESH,
        )

    def to_left():
        return pltpu.make_async_remote_copy(
            kv_hbm, halo.at[1], send_sem.at[1], recv_sem.at[1],
            device_id={"seq": me - 1}, device_id_type=MESH,
        )

    @pl.when(has_right)
    def _():
        to_right().start()

    @pl.when(has_left)
    def _():
        to_left().start()

    ones = jnp.ones((TOTALS, rows), jnp.bfloat16)

    loads[0].wait()
    spread(kv[:, :wide] * scaled, kv[:, wide:].T, ones, kx, vt, 0)
    loads[1].wait()
    key = lax.broadcasted_iota(jnp.int32, (rows, rows), 0)
    query = lax.broadcasted_iota(jnp.int32, (rows, rows), 1)
    apart = jnp.abs(key - query)
    heads = list(range(2 * pairs))

    def queries_of(h):
        pair = h // 2
        return q[:, pair * wide : (pair + 1) * wide]

    def put(h, share, halves, here):
        halves.append(share)
        if h % 2:
            both = jnp.concatenate(halves, axis=0).astype(jnp.bfloat16)
            att[here, h // 2 * wide : (h // 2 + 1) * wide] = both.T
            halves.clear()

    def own_scores(h):
        return dot_nt(kx[0, h // 2 // per_group, h % 2], queries_of(h))

    def own_weigh(h, scores):
        scores = jnp.where(apart <= extent[h], scores, HIDE)
        top = col_max([scores])
        tops[h] = jnp.broadcast_to(top, tops.shape[1:])
        return (weight(scores, top),)

    def own_finish(h, shares):
        accs[h] = dot(vt[0, h // 2 // per_group], shares)

    staggered(heads, own_scores, own_weigh, own_finish)

    @pl.when(has_left)
    def _():
        to_right().wait_recv()

    @pl.when(jnp.logical_not(has_left))
    def _():
        halo[0] = jnp.zeros(halo.shape[1:], jnp.bfloat16)

    @pl.when(has_right)
    def _():
        to_left().wait_recv()

    @pl.when(jnp.logical_not(has_right))
    def _():
        halo[1] = jnp.zeros(halo.shape[1:], jnp.bfloat16)

    for side in range(2):
        spread(halo[side, :, :wide] * scaled, halo[side, :, wide:].T, ones, kx, vt, 1 + side)
    far = 4 * n * rows
    left_off = rows + jnp.where(has_left, 0, far)
    right_off = rows + jnp.where(has_right, 0, far)
    tiles = rows // wide
    for i in (2, 3, 4):
        loads[i].wait()
    swaps = [
        [
            pltpu.make_async_remote_copy(
                kv2.at[pl.ds(tile * 2 * wide, 2 * wide)],
                kv2_in.at[level, pl.ds(tile * 2 * wide, 2 * wide)],
                send_sem.at[2 + level * tiles + tile],
                recv_sem.at[2 + level * tiles + tile],
                device_id={"seq": partner(level)}, device_id_type=MESH,
            )
            for tile in range(tiles)
        ]
        for level in range(levels)
    ]
    halves, normed, turned = [], [], []
    for tile in range(tiles):
        here = slice(tile * wide, (tile + 1) * wide)
        left = slice(tile * wide, rows)
        right = slice(0, (tile + 1) * wide)
        left_apart = (query - key)[left, here] + left_off
        right_apart = (key - query)[right, here] + right_off

        def side_scores(h):
            pair = h // 2
            queries = q[here, pair * wide : (pair + 1) * wide]
            return [
                dot_nt(kx[1, pair // per_group, h % 2, left], queries),
                dot_nt(kx[2, pair // per_group, h % 2, right], queries),
            ]

        def side_weigh(h, parts):
            a = jnp.where(left_apart <= extent[h], parts[0], HIDE)
            b = jnp.where(right_apart <= extent[h], parts[1], HIDE)
            before = tops[h, 0:1, here]
            top = jnp.maximum(before, col_max([a, b]))
            return jnp.exp(before - top), weight(a, top), weight(b, top)

        def side_finish(h, fade, a, b):
            acc = accs[h, :, here] * fade
            acc += dot(vt[1, h // 2 // per_group, :, left], a)
            acc += dot(vt[2, h // 2 // per_group, :, right], b)
            put(h, shared(acc), halves, here)

        staggered(heads, side_scores, side_weigh, side_finish)

        hidden = (dot(att[here], wo1[...]) + res[here].astype(jnp.float32)).astype(jnp.bfloat16)
        hid[here] = hidden
        values = hidden.astype(jnp.float32)
        scale = lax.rsqrt(jnp.mean(values * values, axis=-1, keepdims=True) + 1e-05)
        normed.append((values * scale).astype(jnp.bfloat16))
        keyvals = dot(normed[-1], wkv2[...]).astype(jnp.bfloat16)
        turned.append(keyvals[:, wide:].T)
        kv2[tile * 2 * wide : (tile * 2 + 1) * wide] = keyvals[:, :wide] * scaled
        kv2[(tile * 2 + 1) * wide : (tile * 2 + 2) * wide] = turned[-1]
        for swap in swaps:
            swap[tile].start()

    def keys_of(block):
        return jnp.concatenate([block[2 * t * wide : (2 * t + 1) * wide] for t in range(tiles)], axis=0)

    def values_of(block):
        return jnp.concatenate(
            [block[(2 * t + 1) * wide : (2 * t + 2) * wide] for t in range(tiles)], axis=1
        )

    keep_hidden = pltpu.make_async_copy(hid, hid_out, local_sem.at[6])
    keep_hidden.start()
    loads[5].wait()
    q[...] = dot(jnp.concatenate(normed, axis=0), wq2[...]).astype(jnp.bfloat16)
    spread(keys_of(kv2), values_of(kv2), ones, kx, vt, 0)

    blocks = [[(slot, tile) for tile in range(tiles)] for slot in range(levels + 1)]
    chunks, first = [], 0
    while first <= levels:
        size = 2 if first + 1 < levels else 1
        chunks.append(sum(blocks[first : first + size], []))
        first += size
    if len(chunks) > 1:
        chunks[-2] += chunks[-1][:-1]
        chunks[-1] = chunks[-1][-1:]
    for chunk in chunks:
        final = chunk is chunks[-1]
        for slot, tile in chunk:
            if slot > 0:
                swaps[slot - 1][tile].wait_recv()
                seen = mask[0, slot - 1] == 1
                here = slice(tile * wide, (tile + 1) * wide)
                at = slice(2 * tile * wide, (2 * tile + 1) * wide)
                came = kv2_in[slot - 1, (2 * tile + 1) * wide : (2 * tile + 2) * wide]
                total = ones[:, :wide]
                spread(
                    jnp.where(seen, kv2_in[slot - 1, at], kv2[at]),
                    jnp.where(seen, came, jnp.zeros_like(came)),
                    jnp.where(seen, total, jnp.zeros_like(total)),
                    kx, vt, slot, here,
                )
        spans = []
        for slot in dict.fromkeys(slot for slot, tile in chunk):
            held = [tile for at, tile in chunk if at == slot]
            spans.append((slot, slice(held[0] * wide, (held[-1] + 1) * wide)))

        def far_scores(h):
            return [dot_nt(kx[slot, h // 2 // per_group, h % 2, span], queries_of(h)) for slot, span in spans]

        def far_weigh(h, parts):
            top = col_max(parts)
            fade = None
            if chunk is not chunks[0]:
                before = tops[h, 0:1]
                top = jnp.maximum(before, top)
                fade = jnp.exp(before - top)
            if not final:
                tops[h] = jnp.broadcast_to(top, tops.shape[1:])
            return fade, [weight(part, top) for part in parts]

        def far_finish(h, fade, parts):
            acc = None if fade is None else accs[h] * fade
            for (slot, span), part in zip(spans, parts):
                term = dot(vt[slot, h // 2 // per_group, :, span], part)
                acc = term if acc is None else acc + term
            if not final:
                accs[h] = acc
            else:
                put(h, shared(acc), halves, slice(0, rows))

        staggered(heads, far_scores, far_weigh, far_finish)

    keep_att = pltpu.make_async_copy(att, att_out, local_sem.at[7])
    keep_att.start()
    for level in swaps:
        for swap in level:
            swap.wait_send()

    @pl.when(has_right)
    def _():
        to_right().wait_send()

    @pl.when(has_left)
    def _():
        to_left().wait_send()

    keep_hidden.wait()
    keep_att.wait()


def shards(
    n, residual, layer_queries, layer_keyvals, head_window_extent, block_mask,
    first_out, second_query, second_keyval, second_out,
):
    levels = n.bit_length() - 1
    rows, width = residual.shape
    query_width = layer_queries.shape[1]
    kv_width = layer_keyvals.shape[1]
    wide = 2 * HEAD_SIZE
    blocks = max(3, levels + 1)
    bf16, f32 = jnp.bfloat16, jnp.float32
    anywhere = pl.BlockSpec(memory_space=pl.ANY)
    stays = pl.BlockSpec(memory_space=pltpu.HBM)
    scalars = pl.BlockSpec(memory_space=pltpu.SMEM)
    att, hidden = pl.pallas_call(
        functools.partial(body, n, levels),
        name="two_layers",
        out_shape=(
            jax.ShapeDtypeStruct((rows, query_width), bf16),
            jax.ShapeDtypeStruct((rows, width), bf16),
        ),
        in_specs=[stays] * 3 + [scalars] * 2 + [stays] * 3,
        out_specs=(anywhere, anywhere),
        scratch_shapes=[
            pltpu.VMEM((rows, query_width), bf16),
            pltpu.VMEM((rows, kv_width), bf16),
            pltpu.VMEM((2, rows, kv_width), bf16),
            pltpu.VMEM((rows, width), bf16),
            pltpu.VMEM(first_out.shape, bf16),
            pltpu.VMEM(second_query.shape, bf16),
            pltpu.VMEM(second_keyval.shape, bf16),
            pltpu.VMEM((2 * rows, wide), bf16),
            pltpu.VMEM((levels, 2 * rows, wide), bf16),
            pltpu.VMEM((blocks, 2, 2, rows, wide), bf16),
            pltpu.VMEM((blocks, 2, HEAD_SIZE + TOTALS, rows), bf16),
            pltpu.VMEM((QUERY_HEADS, 8, rows), f32),
            pltpu.VMEM((QUERY_HEADS, HEAD_SIZE + TOTALS, rows), f32),
            pltpu.VMEM((rows, query_width), bf16),
            pltpu.VMEM((rows, width), bf16),
            pltpu.SemaphoreType.DMA((8,)),
            pltpu.SemaphoreType.DMA((2 + levels * (rows // wide),)),
            pltpu.SemaphoreType.DMA((2 + levels * (rows // wide),)),
        ],
        compiler_params=pltpu.CompilerParams(
            collective_id=0, has_side_effects=True
        ),
    )(
        layer_queries, layer_keyvals, residual, head_window_extent, block_mask,
        first_out, second_query, second_keyval,
    )
    output = jnp.dot(att, second_out, preferred_element_type=f32) + hidden.astype(f32)
    return output.astype(bf16)


def solution(mesh):
    placed = (
        P(("groups", "seq"), None),
        P(("groups", "seq"), None),
        P(("groups", "seq"), None),
        P(),
        P("seq", None),
        P(),
        P(),
        P(),
        P(),
    )
    return jax.shard_map(
        functools.partial(shards, mesh.shape["seq"]),
        mesh=mesh, in_specs=placed, out_specs=P(("groups", "seq"), None), check_vma=False,
    )
```
